1024 devices in a mesh: lb: 16 (over x, core), rb: 8 (over z), rep: 8 (over y).
Axes of the slice: x: 8, y: 8, z: 8, core: 2. Of those that a mesh axis runs over, the one named last changes fastest.
Arguments:
- left_factor: bfloat16 [1024, 1024], P('lb', 'rep'), may hold values from -5 to 5
- boundary_site: bfloat16 [1024, 16, 1024], P('rep', None, 'rb'), may hold values from -6 to 6
- double_layer: float32 [16, 16], replicated, may hold values from -1.5 to 1.5
Outputs:
- site_q: float32 [16, 1024, 1024], P('rep', 'lb', 'rb')
- factor: float32 [1024, 1024], P('lb')
The draws below stay inside these ranges and needn't reach their ends.
All inputs are finite; a program needn't handle non-finite values.
Results may differ from the reference program's by a relative error of at most 0.0032.
Values sent between devices are 32-bit elements; how exact they have to be, the bound alone decides.
A program may use at most 64 MiB of HBM per device.

```python
import math
import jax
import jax.numpy as jnp
from jax import lax

CHI = 1024
PHYS = 16


def draw_left_factor(key, part):
    first = jax.random.fold_in(key, 11)
    noise = jax.random.normal(first, (CHI, CHI), jnp.float32) * (0.6 / math.sqrt(CHI))
    matrix = jnp.eye(CHI, dtype=jnp.float32) + noise
    return matrix.astype(jnp.bfloat16)


def shard_levels(own_key, dims, cuts, least, largest):
    def one(axis_at, shards_of):
        draws = jax.random.uniform(jax.random.fold_in(jax.random.fold_in(own_key, 6), axis_at), (shards_of,), jnp.float32, least / len(cuts), largest / len(cuts))
        return jnp.repeat(jnp.exp(draws), dims[axis_at] // shards_of).reshape((-1,) + (1,) * (len(dims) - axis_at - 1))

    loudness = one(*cuts[0])
    for cut in cuts[1:]:
        loudness = loudness * one(*cut)
    return loudness


def bell_draw(own_key, extent, deviation, most, pieces=(), kind=jnp.bfloat16):
    level = shard_levels(own_key, extent, pieces, -0.22, 0.18) if pieces else 1.0
    values = jax.random.normal(own_key, extent, jnp.float32) * deviation * level
    return jnp.minimum(jnp.maximum(values, -most), most).astype(kind)


def setup_inputs(seed: int = 0) -> dict:
    keys = jax.random.split(jax.random.key(seed), 4)
    left_factor = draw_left_factor(jax.random.fold_in(keys[3], 71), 0)
    boundary_site = bell_draw(keys[1], (CHI, PHYS, CHI), 1.0, 6.0, ((0, 8), (2, 8)))
    double_layer = bell_draw(keys[2], (PHYS, PHYS), PHYS ** -0.5, 1.5, (), jnp.float32)
    return {"left_factor": left_factor, "boundary_site": boundary_site, "double_layer": double_layer}


def reference(left_factor, boundary_site, double_layer):
    hp = lax.Precision.HIGHEST
    absorbed = jnp.einsum('kur,ue->ker', boundary_site.astype(jnp.float32), double_layer, precision=hp).astype(jnp.bfloat16)
    grown = jnp.einsum('ik,ker->eir', left_factor.astype(jnp.float32), absorbed.astype(jnp.float32), precision=hp)
    gram = jnp.einsum('eir,ejr->ij', grown, grown, precision=hp)
    lower = jnp.linalg.cholesky(gram)
    matrix = jnp.transpose(grown, (1, 0, 2)).reshape(CHI, PHYS * CHI)
    solved = jax.scipy.linalg.solve_triangular(lower, matrix, lower=True)
    scale = math.sqrt(PHYS * CHI)
    site_q = jnp.transpose(solved.reshape(CHI, PHYS, CHI), (1, 0, 2)) * scale
    return (site_q, lower / scale)
```

```python
import jax
import jax.numpy as jnp
from jax import lax
from jax.experimental import pallas as pl
from jax.experimental.pallas import tpu as pltpu
from jax.sharding import PartitionSpec as P

CHI = 1024
BLOCK = 128
TILES = BLOCK // 8
F32 = jnp.float32
BF16 = jnp.bfloat16


NT = (((1,), (1,)), ((), ()))
NN = (((1,), (0,)), ((), ()))


def dot(a, b, dims):
    return lax.dot_general(a, b, dims, precision=lax.Precision.HIGHEST, preferred_element_type=F32)


def factor_block(r_ref):
    sub = lax.broadcasted_iota(jnp.int32, (8, BLOCK), 0)

    def spread(tile, row):
        return jnp.broadcast_to(tile[row : row + 1, :], (8, BLOCK))

    for t in range(TILES):
        at = pl.ds(8 * t, 8)
        left, right = r_ref[at, :BLOCK], r_ref[at, BLOCK:]
        cols = [jnp.broadcast_to(left[:, 8 * t + n : 8 * t + n + 1], (8, BLOCK)) for n in range(8)]
        roots, lefts, rights, links = [], [], [], []
        scale = jnp.zeros((8, BLOCK), F32)
        for i in range(8):
            root = lax.rsqrt(spread(cols[i], i))
            scale = jnp.where(sub == i, root, scale)
            below = jnp.where(sub > i, cols[i] * root, 0.0)
            ul, ur = spread(left, i) * root, spread(right, i) * root
            link = {n: spread(cols[n], i) * root for n in range(i + 1, 8)}
            for n in range(i + 1, 8):
                cols[n] = cols[n] - below * link[n]
            left, right = left - below * ul, right - below * ur
            roots.append(root)
            lefts.append(ul)
            rights.append(ur)
            links.append(link)
        r_ref[at, :BLOCK] = left * scale
        r_ref[at, BLOCK:] = right * scale
        for s in range(t + 1, TILES):
            low = pl.ds(8 * s, 8)
            left, right = r_ref[low, :BLOCK], r_ref[low, BLOCK:]
            cols = [jnp.broadcast_to(left[:, 8 * t + n : 8 * t + n + 1], (8, BLOCK)) for n in range(8)]
            for i in range(8):
                below = cols[i] * roots[i]
                for n in range(i + 1, 8):
                    cols[n] = cols[n] - below * links[i][n]
                left, right = left - below * lefts[i], right - below * rights[i]
            r_ref[low, :BLOCK] = left
            r_ref[low, BLOCK:] = right


def factor_kernel(lb_fn, a_ref, g_ref, q_ref, f_ref, r_ref):
    blocks = CHI // BLOCK
    row = lax.broadcasted_iota(jnp.int32, (BLOCK, BLOCK), 0)
    col = lax.broadcasted_iota(jnp.int32, (BLOCK, BLOCK), 1)

    def body(j, carry):
        here = pl.ds(pl.multiple_of(j * BLOCK, BLOCK), BLOCK)
        r_ref[:, :BLOCK] = a_ref[here, here]
        r_ref[:, BLOCK:] = jnp.where(row == col, 1.0, 0.0).astype(F32)
        factor_block(r_ref)
        for jj in range(blocks):
            @pl.when(j == jj)
            def _():
                lo, hi = jj * BLOCK, (jj + 1) * BLOCK
                inv = jnp.where(row >= col, r_ref[:, BLOCK:], 0.0)
                d = dot(a_ref[lo:hi, lo:hi], inv, NT)
                a_ref[lo:hi, lo:hi] = jnp.where(row >= col, d, 0.0)
                y = []
                for h in range(2):
                    yh = dot(inv, g_ref[h, lo:hi, :], NN)
                    g_ref[h, lo:hi, :] = yh
                    y.append(yh)
                if hi < CHI:
                    a_ref[hi:, lo:hi] = dot(a_ref[hi:, lo:hi], inv, NT)
                for i in range(jj + 1, blocks):
                    mine = pl.ds(i * BLOCK, BLOCK)
                    p = a_ref[mine, lo:hi]
                    a_ref[mine, hi : (i + 1) * BLOCK] -= dot(p, a_ref[hi : (i + 1) * BLOCK, lo:hi], NT)
                    for h in range(2):
                        g_ref[h, mine, :] -= dot(p, y[h], NN)
        return carry

    lax.fori_loop(0, blocks, body, 0)
    lb = lb_fn()
    at = pl.ds(pl.multiple_of(lb * 64, 64), 64)
    for h in range(2):
        q_ref[h] = g_ref[h, at, :] * 128.0
    rr = lb * 64 + lax.broadcasted_iota(jnp.int32, (64, CHI), 0)
    cc = lax.broadcasted_iota(jnp.int32, (64, CHI), 1)
    f_ref[...] = jnp.where(rr >= cc, a_ref[at, :], 0.0) * (1.0 / 128.0)


def factor_call(gram, grown, lb_fn):
    def kernel(a_in, g_in, q_ref, f_ref, a_ref, g_ref, r_ref):
        a_ref[...] = a_in[...]
        g_ref[...] = g_in[...]
        factor_kernel(lb_fn, a_ref, g_ref, q_ref, f_ref, r_ref)

    vm = pl.BlockSpec(memory_space=pltpu.VMEM)
    return pl.pallas_call(
        kernel,
        out_shape=(jax.ShapeDtypeStruct((2, 64, 128), F32), jax.ShapeDtypeStruct((64, CHI), F32)),
        in_specs=[vm, vm],
        out_specs=(vm, vm),
        scratch_shapes=[pltpu.VMEM((CHI, CHI), F32), pltpu.VMEM((2, CHI, 128), F32), pltpu.VMEM((BLOCK, 2 * BLOCK), F32)],
        compiler_params=pltpu.CompilerParams(vmem_limit_bytes=40 << 20),
    )(gram, grown)


def shards(left_factor, boundary_site, double_layer):
    highest = lax.Precision.HIGHEST
    absorbed = jnp.einsum(
        "kur,ue->ker", boundary_site.astype(F32), double_layer, precision=highest
    ).astype(BF16)
    grown_part = lax.psum_scatter(
        jnp.einsum("ik,ker->eir", left_factor, absorbed, preferred_element_type=F32),
        "rep",
        scatter_dimension=0,
        tiled=True,
    )
    grown_all = lax.all_gather(grown_part, "lb", axis=1, tiled=True)
    gram_part = jnp.einsum("eir,ejr->ij", grown_part, grown_all, precision=highest)
    tiles = gram_part.reshape(8, 8, 8, 128).transpose(0, 2, 1, 3).reshape(512, 128)
    tile = lax.psum_scatter(tiles, "rb", scatter_dimension=0, tiled=True)
    tile = lax.psum_scatter(tile, "rep", scatter_dimension=0, tiled=True)
    tiles = lax.all_gather(tile, ("lb", "rb", "rep"), axis=0, tiled=True)
    gram = tiles.reshape(128, 8, 8, 128).transpose(0, 2, 1, 3).reshape(CHI, CHI)
    return factor_call(gram, grown_all, lambda: lax.axis_index("lb"))


def solution(mesh):
    return jax.shard_map(
        shards,
        mesh=mesh,
        in_specs=(P("lb", "rep"), P("rep", None, "rb"), P()),
        out_specs=(P("rep", "lb", "rb"), P("lb", None)),
        check_vma=False,
    )
```

```python
import jax
import jax.numpy as jnp
from jax import lax
from jax.experimental import pallas as pl
from jax.experimental.pallas import tpu as pltpu
from jax.sharding import PartitionSpec as P

CHI = 1024
BLOCK = 128
TILES = BLOCK // 8
F32 = jnp.float32
BF16 = jnp.bfloat16


NT = (((1,), (1,)), ((), ()))
NN = (((1,), (0,)), ((), ()))


def dot(a, b, dims):
    return lax.dot_general(a, b, dims, precision=lax.Precision.HIGHEST, preferred_element_type=F32)


def factor_block(r_ref):
    sub = lax.broadcasted_iota(jnp.int32, (8, BLOCK), 0)

    def spread(tile, row):
        return jnp.broadcast_to(tile[row : row + 1, :], (8, BLOCK))

    for t in range(TILES):
        at = pl.ds(8 * t, 8)
        left, right = r_ref[at, :BLOCK], r_ref[at, BLOCK:]
        cols = [jnp.broadcast_to(left[:, 8 * t + n : 8 * t + n + 1], (8, BLOCK)) for n in range(8)]
        roots, lefts, rights, links = [], [], [], []
        scale = jnp.zeros((8, BLOCK), F32)
        for i in range(8):
            root = lax.rsqrt(spread(cols[i], i))
            scale = jnp.where(sub == i, root, scale)
            below = jnp.where(sub > i, cols[i] * root, 0.0)
            ul, ur = spread(left, i) * root, spread(right, i) * root
            link = {n: spread(cols[n], i) * root for n in range(i + 1, 8)}
            for n in range(i + 1, 8):
                cols[n] = cols[n] - below * link[n]
            left, right = left - below * ul, right - below * ur
            roots.append(root)
            lefts.append(ul)
            rights.append(ur)
            links.append(link)
        r_ref[at, :BLOCK] = left * scale
        r_ref[at, BLOCK:] = right * scale
        for s in range(t + 1, TILES):
            low = pl.ds(8 * s, 8)
            left, right = r_ref[low, :BLOCK], r_ref[low, BLOCK:]
            cols = [jnp.broadcast_to(left[:, 8 * t + n : 8 * t + n + 1], (8, BLOCK)) for n in range(8)]
            for i in range(8):
                below = cols[i] * roots[i]
                for n in range(i + 1, 8):
                    cols[n] = cols[n] - below * links[i][n]
                left, right = left - below * lefts[i], right - below * rights[i]
            r_ref[low, :BLOCK] = left
            r_ref[low, BLOCK:] = right


def factor_kernel(lb_fn, a_ref, g_ref, q_ref, f_ref, r_ref):
    blocks = CHI // BLOCK
    row = lax.broadcasted_iota(jnp.int32, (BLOCK, BLOCK), 0)
    col = lax.broadcasted_iota(jnp.int32, (BLOCK, BLOCK), 1)

    def body(j, carry):
        here = pl.ds(pl.multiple_of(j * BLOCK, BLOCK), BLOCK)
        r_ref[:, :BLOCK] = a_ref[here, here]
        r_ref[:, BLOCK:] = jnp.where(row == col, 1.0, 0.0).astype(F32)
        factor_block(r_ref)
        for jj in range(blocks):
            @pl.when(j == jj)
            def _():
                lo, hi = jj * BLOCK, (jj + 1) * BLOCK
                inv = jnp.where(row >= col, r_ref[:, BLOCK:], 0.0)
                d = dot(a_ref[lo:hi, lo:hi], inv, NT)
                a_ref[lo:hi, lo:hi] = jnp.where(row >= col, d, 0.0)
                y = []
                for h in range(2):
                    yh = dot(inv, g_ref[h, lo:hi, :], NN)
                    g_ref[h, lo:hi, :] = yh
                    y.append(yh)
                if hi < CHI:
                    a_ref[hi:, lo:hi] = dot(a_ref[hi:, lo:hi], inv, NT)
                for i in range(jj + 1, blocks):
                    mine = pl.ds(i * BLOCK, BLOCK)
                    p = a_ref[mine, lo:hi]
                    a_ref[mine, hi : (i + 1) * BLOCK] -= dot(p, a_ref[hi : (i + 1) * BLOCK, lo:hi], NT)
                    for h in range(2):
                        g_ref[h, mine, :] -= dot(p, y[h], NN)
        return carry

    lax.fori_loop(0, blocks, body, 0)
    lb = lb_fn()
    at = pl.ds(pl.multiple_of(lb * 64, 64), 64)
    for h in range(2):
        q_ref[h] = g_ref[h, at, :] * 128.0
    rr = lb * 64 + lax.broadcasted_iota(jnp.int32, (64, CHI), 0)
    cc = lax.broadcasted_iota(jnp.int32, (64, CHI), 1)
    f_ref[...] = jnp.where(rr >= cc, a_ref[at, :], 0.0) * (1.0 / 128.0)


MESH = pl.DeviceIdType.MESH


def mod(value, size):
    return lax.rem(value + 2 * size, size)


def gather_kernel(sizes, part_ref, grown_ref, gram_ref, a_recv, products, z_recv, total, y_recv, tile, sems):
    nx, nz, ny = sizes
    lb, z, y = lax.axis_index("lb"), lax.axis_index("rb"), lax.axis_index("rep")
    x, core = lb // 2, lax.rem(lb, 2)
    half = nx // 2
    (a_send, a_got, b_send, b_got, p_send, p_got, c_send, c_got, d_send, d_got,
     e_send, e_got, f_send, f_got, g_send, g_got, h_send, h_got) = sems

    def remote(src, dst, send, got, target):
        return pltpu.make_async_remote_copy(
            src_ref=src, dst_ref=dst, send_sem=send, recv_sem=got, device_id=target, device_id_type=MESH
        )

    barrier = pltpu.get_barrier_semaphore()
    for d in range(1, ny):
        pl.semaphore_signal(barrier, inc=1, device_id={"rep": mod(y + d, ny)}, device_id_type=MESH)
    for d in range(1, nz):
        pl.semaphore_signal(barrier, inc=1, device_id={"rb": mod(z + d, nz)}, device_id_type=MESH)
    for d in range(1, 2 * nx):
        pl.semaphore_signal(barrier, inc=1, device_id={"lb": mod(lb + d, 2 * nx)}, device_id_type=MESH)
    pl.semaphore_wait(barrier, ny - 1 + nz - 1 + 2 * nx - 1)

    def far_first(n):
        return sorted(range(1, n), key=lambda d: -min(d, n - d))

    copies = []
    for d in far_first(ny):
        to = mod(y + d, ny)
        copy = remote(part_ref.at[pl.ds(2 * to, 2)], a_recv.at[d - 1], a_send.at[d - 1], a_got.at[d - 1], {"rep": to})
        copy.start()
        copies.append(copy)
    mine = part_ref[pl.ds(2 * y, 2)]
    for copy, d in sorted(zip(copies, far_first(ny)), key=lambda pair: min(pair[1], ny - pair[1])):
        copy.wait_recv()
        mine = mine + a_recv[d - 1]
    rows = pl.ds(pl.multiple_of(lb * 64, 64), 64)
    for e in range(2):
        grown_ref[e, rows, :] = mine[e]
    sent = list(copies)

    def block(e, chip, which):
        return grown_ref.at[e, pl.ds(pl.multiple_of((2 * chip + which) * 64, 64), 64)]

    partner = {"lb": 2 * x + 1 - core}
    handed = []

    def hand(e, chip, slot):
        copy = remote(block(e, chip, core), block(e, chip, core), p_send.at[slot], p_got.at[slot], partner)
        copy.start()
        handed.append(copy)

    def ring(direction, step, e):
        chip = mod(x - direction * (step - 1), nx)
        side = 0 if direction > 0 else 1
        slot = (side * half + step - 1) * 2 + e
        to = {"lb": 2 * mod(x + direction, nx) + core}
        copy = remote(block(e, chip, core), block(e, chip, core), b_send.at[slot], b_got.at[slot], to)
        copy.start()
        sent.append(copy)
        return copy

    def moves(step):
        full = [(direction, e) for e in range(2) for direction in (1, -1)]
        return full if step < half else [(1, 0), (-1, 1)]

    flying = {}
    for direction, e in moves(1):
        flying[direction, 1, e] = ring(direction, 1, e)
    for e in range(2):
        hand(e, x, e)
    slot = 2
    for step in range(1, half + 1):
        for direction, e in moves(step):
            flying[direction, step, e].wait_recv()
            if step < half and (direction, e) in moves(step + 1):
                flying[direction, step + 1, e] = ring(direction, step + 1, e)
            hand(e, mod(x - direction * step, nx), slot)
            slot += 1
    for copy in handed:
        copy.wait_recv()
    sent += handed

    ours = [grown_ref[e, rows, :] for e in range(2)]
    copies = []
    for d in far_first(nz) + [0]:
        to = mod(z + d, nz)
        at = pl.ds(pl.multiple_of(to * 128, 128), 128)
        products[d] = dot(ours[0], grown_ref[0, at, :], NT) + dot(ours[1], grown_ref[1, at, :], NT)
        if d:
            copy = remote(products.at[d], z_recv.at[d - 1], c_send.at[d - 1], c_got.at[d - 1], {"rb": to})
            copy.start()
            copies.append((d, copy))
    summed = products[0]
    for d, copy in sorted(copies, key=lambda pair: min(pair[0], nz - pair[0])):
        copy.wait_recv()
        summed = summed + z_recv[d - 1]
    total[...] = summed
    sent += [copy for _, copy in copies]
    copies = []
    for d in far_first(ny):
        to = mod(y + d, ny)
        src = total.at[pl.ds(pl.multiple_of(8 * to, 8), 8)]
        copy = remote(src, y_recv.at[d - 1], d_send.at[d - 1], d_got.at[d - 1], {"rep": to})
        copy.start()
        copies.append((d, copy))
    summed = total[pl.ds(pl.multiple_of(8 * y, 8), 8), :]
    for d, copy in sorted(copies, key=lambda pair: min(pair[0], ny - pair[0])):
        copy.wait_recv()
        summed = summed + y_recv[d - 1]
    tile[...] = summed
    sent += [copy for _, copy in copies]

    def place(which):
        return z * (1 - which) + y * which, y * (1 - which) + z * which

    side = lb // nx
    outer, inner = place(side)
    spot = lax.rem(lb, nx)
    home = gram_ref.at[side, outer, inner, pl.ds(pl.multiple_of(8 * spot, 8), 8)]
    copies = []
    for d in far_first(nx):
        copy = remote(tile, home, e_send.at[d], e_got.at[spot], {"lb": 2 * mod(x + d, nx) + side})
        copy.start()
        copies.append(copy)
    across = remote(tile, home, e_send.at[0], e_got.at[spot], partner)
    here = pltpu.make_async_copy(tile, home, e_got.at[spot])

    @pl.when(core == side)
    def _():
        here.start()

    @pl.when(core != side)
    def _():
        across.start()
        across.wait_send()

    sent += copies
    outer, inner = place(core)
    for i in range(nx):
        landed = gram_ref.at[core, outer, inner, pl.ds(8 * i, 8)]
        pltpu.make_async_copy(tile, landed, e_got.at[i]).wait()

    n = ny
    copies = []
    chunk = gram_ref.at[core, outer, inner]
    for d in far_first(n):
        to = {"rep": mod(y + d * (1 - core), n), "rb": mod(z + d * core, n)}
        copy = remote(chunk, chunk, f_send.at[d - 1], f_got.at[d - 1], to)
        copy.start()
        copies.append(copy)
    for copy in copies:
        copy.wait_recv()
    sent += copies

    cuts = 4
    width = n // cuts
    middle = n // 2

    def piece(position, cut):
        return gram_ref.at[core, position, pl.ds(cut * width, width)]

    def around(direction, step, cut):
        position = mod(outer - direction * (step - 1), n)
        slot = ((0 if direction > 0 else 1) * middle + step - 1) * cuts + cut
        to = {"rb": mod(z + direction * (1 - core), n), "rep": mod(y + direction * core, n)}
        copy = remote(piece(position, cut), piece(position, cut), g_send.at[slot], g_got.at[slot], to)
        copy.start()
        sent.append(copy)
        return copy

    handed = []

    def share(position, cut, slot):
        copy = remote(piece(position, cut), piece(position, cut), h_send.at[slot], h_got.at[slot], partner)
        copy.start()
        handed.append(copy)

    def turns(step):
        if step < middle:
            return [(direction, cut) for cut in range(cuts) for direction in (1, -1)]
        return [(1 if cut < cuts // 2 else -1, cut) for cut in (0, cuts // 2, 1, cuts // 2 + 1)]

    flying = {}
    for direction, cut in turns(1):
        flying[direction, 1, cut] = around(direction, 1, cut)
    for cut in range(cuts):
        share(outer, cut, cut)
    slot = cuts
    for step in range(1, middle + 1):
        for direction, cut in turns(step):
            flying[direction, step, cut].wait_recv()
            if step < middle and (direction, cut) in turns(step + 1):
                flying[direction, step + 1, cut] = around(direction, step + 1, cut)
            share(mod(outer - direction * step, n), cut, slot)
            slot += 1
    for copy in handed:
        copy.wait_recv()
    for copy in sent + handed:
        copy.wait_send()


def gather_call(part, sizes):
    nx, nz, ny = sizes
    vm = pl.BlockSpec(memory_space=pltpu.VMEM)
    counts = [ny - 1] * 2 + [2 * nx] * 4 + [nz - 1] * 2 + [ny - 1] * 2 + [nx] * 2 + [ny - 1] * 2 + [4 * ny] * 4

    def kernel(part_ref, grown_ref, gram_ref, a_recv, products, z_recv, total, y_recv, tile, *sems):
        gather_kernel(sizes, part_ref, grown_ref, gram_ref, a_recv, products, z_recv, total, y_recv, tile, sems)

    return pl.pallas_call(
        kernel,
        out_shape=(
            jax.ShapeDtypeStruct((2, 128 * nx, 128), F32),
            jax.ShapeDtypeStruct((2, ny, ny, 8 * nx, 128), F32),
        ),
        in_specs=[vm],
        out_specs=(vm, vm),
        scratch_shapes=[
            pltpu.VMEM((ny - 1, 2, 64, 128), F32),
            pltpu.VMEM((nz, 64, 128), F32),
            pltpu.VMEM((nz - 1, 64, 128), F32),
            pltpu.VMEM((64, 128), F32),
            pltpu.VMEM((ny - 1, 8, 128), F32),
            pltpu.VMEM((8, 128), F32),
        ]
        + [pltpu.SemaphoreType.DMA((count,)) for count in counts],
        compiler_params=pltpu.CompilerParams(collective_id=0, has_side_effects=True, vmem_limit_bytes=24 << 20),
    )(part)


def factor_call(gram, grown, lb_fn):
    def kernel(a_in, g_in, q_ref, f_ref, a_ref, g_ref, r_ref):
        for outer in range(8):
            for inner in range(8):
                for i in range(8):
                    at = pl.ds(8 * i, 8)
                    up, low = 64 * i + 8 * inner, 512 + 64 * i + 8 * outer
                    a_ref[up : up + 8, 128 * outer : 128 * outer + 128] = a_in[0, outer, inner, at, :]
                    a_ref[low : low + 8, 128 * inner : 128 * inner + 128] = a_in[1, outer, inner, at, :]
        g_ref[...] = g_in[...]
        factor_kernel(lb_fn, a_ref, g_ref, q_ref, f_ref, r_ref)

    vm = pl.BlockSpec(memory_space=pltpu.VMEM)
    return pl.pallas_call(
        kernel,
        out_shape=(jax.ShapeDtypeStruct((2, 64, 128), F32), jax.ShapeDtypeStruct((64, CHI), F32)),
        in_specs=[vm, vm],
        out_specs=(vm, vm),
        scratch_shapes=[pltpu.VMEM((CHI, CHI), F32), pltpu.VMEM((2, CHI, 128), F32), pltpu.VMEM((BLOCK, 2 * BLOCK), F32)],
        compiler_params=pltpu.CompilerParams(vmem_limit_bytes=24 << 20),
    )(gram, grown)


def shards(left_factor, boundary_site, double_layer):
    highest = lax.Precision.HIGHEST
    absorbed = jnp.einsum(
        "kur,ue->ker", boundary_site.astype(F32), double_layer, precision=highest
    ).astype(BF16)
    part = jnp.einsum("ik,ker->eir", left_factor, absorbed, preferred_element_type=F32)
    grown, gram = gather_call(part, (8, 8, 8))
    return factor_call(gram, grown, lambda: lax.axis_index("lb"))


def solution(mesh):
    return jax.shard_map(
        shards,
        mesh=mesh,
        in_specs=(P("lb", "rep"), P("rep", None, "rb"), P()),
        out_specs=(P("rep", "lb", "rb"), P("lb", None)),
        check_vma=False,
    )
```

```python
import jax
import jax.numpy as jnp
from jax import lax
from jax.experimental import pallas as pl
from jax.experimental.pallas import tpu as pltpu
from jax.sharding import PartitionSpec as P

CHI = 1024
BLOCK = 128
BLOCKS = CHI // BLOCK
TILES = BLOCK // 8
F32 = jnp.float32
BF16 = jnp.bfloat16
NT = (((1,), (1,)), ((), ()))
NN = (((1,), (0,)), ((), ()))


def dot(a, b, dims):
    return lax.dot_general(a, b, dims, precision=lax.Precision.HIGHEST, preferred_element_type=F32)


def mul(a, b, dims):
    return lax.dot_general(a, b, dims, preferred_element_type=F32)


def split(x):
    high = x.astype(BF16)
    rest = x - high.astype(F32)
    middle = rest.astype(BF16)
    return high, middle, (rest - middle.astype(F32)).astype(BF16)


def first(x):
    h, m, l = split(x)
    return jnp.concatenate([h, h, m, m, h, l], axis=1)


def second(x, axis):
    h, m, l = split(x)
    return jnp.concatenate([h, m, h, m, l, h], axis=axis)


def factor_block(r_ref, shadows):
    sub = lax.broadcasted_iota(jnp.int32, (8, BLOCK), 0)
    shadows = list(shadows)
    share = -(-len(shadows) // TILES)

    def spread(tile, row):
        return jnp.broadcast_to(tile[row : row + 1, :], (8, BLOCK))

    for t in range(TILES):
        at = pl.ds(8 * t, 8)
        left, right = r_ref[at, :BLOCK], r_ref[at, BLOCK:]
        cols = [jnp.broadcast_to(left[:, 8 * t + n : 8 * t + n + 1], (8, BLOCK)) for n in range(8)]
        roots, lefts, rights, links = [], [], [], []
        scale = jnp.zeros((8, BLOCK), F32)
        for i in range(8):
            root = lax.rsqrt(spread(cols[i], i))
            scale = jnp.where(sub == i, root, scale)
            below = jnp.where(sub > i, cols[i] * root, 0.0)
            ul, ur = spread(left, i) * root, spread(right, i) * root
            link = {n: spread(cols[n], i) * root for n in range(i + 1, 8)}
            for n in range(i + 1, 8):
                cols[n] = cols[n] - below * link[n]
            left, right = left - below * ul, right - below * ur
            roots.append(root)
            lefts.append(ul)
            rights.append(ur)
            links.append(link)
        r_ref[at, BLOCK:] = right * scale
        for s in range(t + 1, TILES):
            low = pl.ds(8 * s, 8)
            left, right = r_ref[low, :BLOCK], r_ref[low, BLOCK:]
            cols = [jnp.broadcast_to(left[:, 8 * t + n : 8 * t + n + 1], (8, BLOCK)) for n in range(8)]
            for i in range(8):
                below = cols[i] * roots[i]
                for n in range(i + 1, 8):
                    cols[n] = cols[n] - below * links[i][n]
                left, right = left - below * lefts[i], right - below * rights[i]
            r_ref[low, :BLOCK] = left
            r_ref[low, BLOCK:] = right
        for shadow in shadows[t * share : (t + 1) * share]:
            shadow()


def factor_kernel(lb_fn, a_ref, g_ref, q_ref, f_ref, r_ref, c_ref, pa_ref, pb_ref, y_ref, ia_ref, ib_ref):
    row = lax.broadcasted_iota(jnp.int32, (BLOCK, BLOCK), 0)
    col = lax.broadcasted_iota(jnp.int32, (BLOCK, BLOCK), 1)
    one = jnp.where(row == col, 1.0, 0.0).astype(F32)

    def block(j):
        return pl.ds(pl.multiple_of(j * BLOCK, BLOCK), BLOCK)

    def chunk(i):
        return slice(256 * i, 256 * i + 256)

    def keep_inverse():
        inv = jnp.where(row >= col, r_ref[:, BLOCK:], 0.0)
        ia_ref[...] = first(inv)
        ib_ref[...] = second(inv, 1)

    def column(j, i):
        def run():
            p = mul(c_ref[chunk(i), :], ib_ref[...], NT)
            rows = 256 * i + lax.broadcasted_iota(jnp.int32, (256, BLOCK), 0)
            cols = j * BLOCK + lax.broadcasted_iota(jnp.int32, (256, BLOCK), 1)
            a_ref[chunk(i), block(j)] = jnp.where(rows >= cols, p, 0.0)
            h, m, l = split(jnp.where(rows >= (j + 1) * BLOCK, p, 0.0))
            pa_ref[chunk(i), :] = jnp.concatenate([h, h, m, m, h, l], axis=1)
            pb_ref[chunk(i), :] = jnp.concatenate([h, m, h, m, l, h], axis=1)
        return run

    def solve(j, h):
        def run():
            y = mul(ia_ref[...], second(g_ref[h, block(j), :], 0), NN)
            g_ref[h, block(j), :] = y
            y_ref[h] = second(y, 0)
        return run

    def ahead(j, i):
        def run():
            c = a_ref[chunk(i), block(j + 1)] - mul(pa_ref[chunk(i), :], pb_ref[block(j + 1), :], NT)
            c_ref[chunk(i), :] = first(c)
        return run

    def trail(k, i):
        def run():
            lo = max(256 * i, BLOCK * k)
            rows = slice(lo, 256 * i + 256)
            cols = slice(BLOCK * k, BLOCK * k + BLOCK)
            a_ref[rows, cols] -= mul(pa_ref[rows, :], pb_ref[cols, :], NT)
        return run

    def sweep(h, i):
        def run():
            at = slice(max(256 * i, BLOCK), 256 * i + 256)
            g_ref[h, at, :] -= mul(pa_ref[at, :], y_ref[h], NN)
        return run

    r_ref[:, :BLOCK] = a_ref[:BLOCK, :BLOCK]
    r_ref[:, BLOCK:] = one
    factor_block(r_ref, [])
    keep_inverse()
    for i in range(4):
        c_ref[chunk(i), :] = first(a_ref[chunk(i), :BLOCK])

    def body(j, carry):
        p = mul(c_ref[block(j + 1), :], ib_ref[...], NT)
        r_ref[:, :BLOCK] = a_ref[block(j + 1), block(j + 1)] - mul(first(p), second(p, 1), NT)
        r_ref[:, BLOCK:] = one
        shadows = [column(j, i) for i in range(4)] + [solve(j, h) for h in range(2)] + [ahead(j, i) for i in range(4)]
        shadows += [trail(k, i) for k in range(2, BLOCKS) for i in range(k // 2, 4)]
        shadows += [sweep(h, i) for h in range(2) for i in range(4)]
        factor_block(r_ref, shadows)
        keep_inverse()
        return carry

    lax.fori_loop(0, BLOCKS - 1, body, 0)
    for i in range(4):
        column(BLOCKS - 1, i)()
    for h in range(2):
        solve(BLOCKS - 1, h)()
    lb = lb_fn()
    at = pl.ds(pl.multiple_of(lb * 64, 64), 64)
    for h in range(2):
        q_ref[h] = g_ref[h, at, :] * 128.0
    f_ref[...] = a_ref[at, :] * (1.0 / 128.0)


SCRATCH = [
    pltpu.VMEM((CHI, CHI), F32),
    pltpu.VMEM((2, CHI, BLOCK), F32),
    pltpu.VMEM((BLOCK, 2 * BLOCK), F32),
    pltpu.VMEM((CHI, 6 * BLOCK), BF16),
    pltpu.VMEM((CHI, 6 * BLOCK), BF16),
    pltpu.VMEM((CHI, 6 * BLOCK), BF16),
    pltpu.VMEM((2, 6 * BLOCK, BLOCK), BF16),
    pltpu.VMEM((BLOCK, 6 * BLOCK), BF16),
    pltpu.VMEM((BLOCK, 6 * BLOCK), BF16),
]


MESH = pl.DeviceIdType.MESH


def mod(value, size):
    return lax.rem(value + 2 * size, size)


def gather_kernel(sizes, part_ref, grown_ref, gram_ref, a_recv, products, z_recv, total, y_recv, tile, sems):
    nx, nz, ny = sizes
    lb, z, y = lax.axis_index("lb"), lax.axis_index("rb"), lax.axis_index("rep")
    x, core = lb // 2, lax.rem(lb, 2)
    half = nx // 2
    (a_send, a_got, b_send, b_got, p_send, p_got, c_send, c_got, d_send, d_got,
     e_send, e_got, f_send, f_got, g_send, g_got, h_send, h_got) = sems

    def remote(src, dst, send, got, target):
        return pltpu.make_async_remote_copy(
            src_ref=src, dst_ref=dst, send_sem=send, recv_sem=got, device_id=target, device_id_type=MESH
        )

    barrier = pltpu.get_barrier_semaphore()
    for d in range(1, ny):
        pl.semaphore_signal(barrier, inc=1, device_id={"rep": mod(y + d, ny)}, device_id_type=MESH)
    for d in range(1, nz):
        pl.semaphore_signal(barrier, inc=1, device_id={"rb": mod(z + d, nz)}, device_id_type=MESH)
    for d in range(1, 2 * nx):
        pl.semaphore_signal(barrier, inc=1, device_id={"lb": mod(lb + d, 2 * nx)}, device_id_type=MESH)
    pl.semaphore_wait(barrier, ny - 1 + nz - 1 + 2 * nx - 1)

    def far_first(n):
        return sorted(range(1, n), key=lambda d: -min(d, n - d))

    rows = pl.ds(pl.multiple_of(lb * 64, 64), 64)
    sent = []

    arriving = {}
    for e in range(2):
        for d in far_first(ny):
            to = mod(y + d, ny)
            at = e * (ny - 1) + d - 1
            copy = remote(part_ref.at[2 * to + e], a_recv.at[at], a_send.at[at], a_got.at[at], {"rep": to})
            copy.start()
            arriving[e, d] = copy
            sent.append(copy)

    def near_first(n):
        return sorted(range(1, n), key=lambda d: min(d, n - d))

    def settle(e):
        mine = part_ref[2 * y + e]
        for d in near_first(ny):
            arriving[e, d].wait_recv()
            mine = mine + a_recv[e * (ny - 1) + d - 1]
        grown_ref[e, rows, :] = mine

    def block(e, chip, which):
        return grown_ref.at[e, pl.ds(pl.multiple_of((2 * chip + which) * 64, 64), 64)]

    partner = {"lb": 2 * x + 1 - core}
    handed = {}

    def hand(e, step, direction):
        chip = mod(x - direction * step, nx)
        slot = ((0 if direction > 0 else 1) * (half + 1) + step) * 2 + e
        copy = remote(block(e, chip, core), block(e, chip, core), p_send.at[slot], p_got.at[slot], partner)
        copy.start()
        handed[direction, step, e] = copy
        sent.append(copy)

    flying = {}

    def ring(direction, step, e):
        chip = mod(x - direction * (step - 1), nx)
        slot = ((0 if direction > 0 else 1) * half + step - 1) * 2 + e
        to = {"lb": 2 * mod(x + direction, nx) + core}
        copy = remote(block(e, chip, core), block(e, chip, core), b_send.at[slot], b_got.at[slot], to)
        copy.start()
        flying[direction, step, e] = copy
        sent.append(copy)

    def ways(step, e):
        return (1, -1) if step < half else ((1,) if e == 0 else (-1,))

    def launch(e):
        for direction in ways(1, e):
            ring(direction, 1, e)
        hand(e, 0, 1)

    def advance(step, e):
        for direction in ways(step, e):
            flying[direction, step, e].wait_recv()
            if step < half and direction in ways(step + 1, e):
                ring(direction, step + 1, e)
            hand(e, step, direction)

    def product(chip):
        at = pl.ds(pl.multiple_of(chip * 128, 128), 128)
        ours = [grown_ref[e, rows, :] for e in range(2)]
        products[chip] = dot(ours[0], grown_ref[0, at, :], NT) + dot(ours[1], grown_ref[1, at, :], NT)

        @pl.when(chip != z)
        def _():
            remote(products.at[chip], z_recv.at[z], c_send.at[chip], c_got.at[z], {"rb": chip}).start()

    settle(0)
    launch(0)
    advance(1, 0)
    settle(1)
    launch(1)
    for e in range(2):
        handed[1, 0, e].wait_recv()
    product(x)
    for step in range(1, half + 1):
        if step > 1:
            advance(step, 0)
        advance(step, 1)
        if step < half:
            for direction in (1, -1):
                for e in range(2):
                    handed[direction, step, e].wait_recv()
                product(mod(x - direction * step, nx))
    handed[1, half, 0].wait_recv()
    handed[-1, half, 1].wait_recv()
    product(mod(x + half, nx))
    summed = products[z]
    for d in near_first(nz):
        far = mod(z + d, nz)
        copy = remote(products.at[far], z_recv.at[far], c_send.at[far], c_got.at[far], {"rb": far})
        copy.wait_recv()
        summed = summed + z_recv[far]
        sent.append(copy)
    total[...] = summed
    copies = []
    for d in far_first(ny):
        to = mod(y + d, ny)
        src = total.at[pl.ds(pl.multiple_of(8 * to, 8), 8)]
        copy = remote(src, y_recv.at[d - 1], d_send.at[d - 1], d_got.at[d - 1], {"rep": to})
        copy.start()
        copies.append((d, copy))
    summed = total[pl.ds(pl.multiple_of(8 * y, 8), 8), :]
    for d, copy in sorted(copies, key=lambda pair: min(pair[0], ny - pair[0])):
        copy.wait_recv()
        summed = summed + y_recv[d - 1]
    tile[...] = summed
    sent += [copy for _, copy in copies]

    def place(which):
        return z * (1 - which) + y * which, y * (1 - which) + z * which

    side = lb // nx
    outer, inner = place(side)
    spot = lax.rem(lb, nx)
    home = gram_ref.at[side, outer, inner, pl.ds(pl.multiple_of(8 * spot, 8), 8)]
    copies = []
    for d in far_first(nx):
        copy = remote(tile, home, e_send.at[d], e_got.at[spot], {"lb": 2 * mod(x + d, nx) + side})
        copy.start()
        copies.append(copy)
    across = remote(tile, home, e_send.at[0], e_got.at[spot], partner)
    here = pltpu.make_async_copy(tile, home, e_got.at[spot])

    @pl.when(core == side)
    def _():
        here.start()

    @pl.when(core != side)
    def _():
        across.start()
        across.wait_send()

    sent += copies
    outer, inner = place(core)
    for i in range(nx):
        landed = gram_ref.at[core, outer, inner, pl.ds(8 * i, 8)]
        pltpu.make_async_copy(tile, landed, e_got.at[i]).wait()

    n = ny
    chunk = gram_ref.at[core, outer, inner]
    for d in far_first(n):
        to = {"rep": mod(y + d * (1 - core), n), "rb": mod(z + d * core, n)}
        copy = remote(chunk, chunk, f_send.at[d], f_got.at[inner], to)
        copy.start()
        sent.append(copy)

    def gathered(position):
        @pl.when(position != inner)
        def _():
            remote(chunk, chunk, f_send.at[0], f_got.at[position], partner).wait_recv()

    cuts = 4
    width = n // cuts
    middle = n // 2

    def piece(position, cut):
        return gram_ref.at[core, position, pl.ds(cut * width, width)]

    def around(direction, step, cut):
        position = mod(outer - direction * (step - 1), n)
        slot = ((0 if direction > 0 else 1) * middle + step - 1) * cuts + cut
        to = {"rb": mod(z + direction * (1 - core), n), "rep": mod(y + direction * core, n)}
        copy = remote(piece(position, cut), piece(position, cut), g_send.at[slot], g_got.at[slot], to)
        copy.start()
        sent.append(copy)
        return copy

    handed = []

    def share(position, cut, slot):
        copy = remote(piece(position, cut), piece(position, cut), h_send.at[slot], h_got.at[slot], partner)
        copy.start()
        handed.append(copy)

    def turns(step):
        if step < middle:
            return [(direction, cut) for cut in range(cuts) for direction in (1, -1)]
        return [(1 if cut < cuts // 2 else -1, cut) for cut in (0, cuts // 2, 1, cuts // 2 + 1)]

    flying = {}
    for cut in range(cuts):
        for position in range(cut * width, cut * width + width):
            gathered(position)
        for direction in (1, -1):
            flying[direction, 1, cut] = around(direction, 1, cut)
        share(outer, cut, cut)
    slot = cuts
    for step in range(1, middle + 1):
        for direction, cut in turns(step):
            flying[direction, step, cut].wait_recv()
            if step < middle and (direction, cut) in turns(step + 1):
                flying[direction, step + 1, cut] = around(direction, step + 1, cut)
            share(mod(outer - direction * step, n), cut, slot)
            slot += 1
    for copy in handed:
        copy.wait_recv()
    for copy in sent + handed:
        copy.wait_send()


def gather_call(part, sizes):
    nx, nz, ny = sizes
    vm = pl.BlockSpec(memory_space=pltpu.VMEM)
    counts = [2 * (ny - 1)] * 2 + [2 * nx] * 2 + [2 * nx + 4] * 2 + [nz] * 2 + [ny - 1] * 2 + [nx] * 2 + [ny] * 2 + [4 * ny] * 4

    def kernel(part_ref, grown_ref, gram_ref, a_recv, products, z_recv, total, y_recv, tile, *sems):
        gather_kernel(sizes, part_ref, grown_ref, gram_ref, a_recv, products, z_recv, total, y_recv, tile, sems)

    return pl.pallas_call(
        kernel,
        out_shape=(
            jax.ShapeDtypeStruct((2, 128 * nx, 128), F32),
            jax.ShapeDtypeStruct((2, ny, ny, 8 * nx, 128), F32),
        ),
        in_specs=[vm],
        out_specs=(vm, vm),
        scratch_shapes=[
            pltpu.VMEM((2 * (ny - 1), 64, 128), F32),
            pltpu.VMEM((nz, 64, 128), F32),
            pltpu.VMEM((nz, 64, 128), F32),
            pltpu.VMEM((64, 128), F32),
            pltpu.VMEM((ny - 1, 8, 128), F32),
            pltpu.VMEM((8, 128), F32),
        ]
        + [pltpu.SemaphoreType.DMA((count,)) for count in counts],
        compiler_params=pltpu.CompilerParams(collective_id=0, has_side_effects=True, vmem_limit_bytes=24 << 20),
    )(part)


def factor_call(gram, grown, lb_fn):
    def kernel(a_in, g_in, q_ref, f_ref, a_ref, g_ref, *scratch):
        for outer in range(8):
            for inner in range(8):
                for i in range(8):
                    at = pl.ds(8 * i, 8)
                    up, low = 64 * i + 8 * inner, 512 + 64 * i + 8 * outer
                    a_ref[up : up + 8, 128 * outer : 128 * outer + 128] = a_in[0, outer, inner, at, :]
                    a_ref[low : low + 8, 128 * inner : 128 * inner + 128] = a_in[1, outer, inner, at, :]
        g_ref[...] = g_in[...]
        factor_kernel(lb_fn, a_ref, g_ref, q_ref, f_ref, *scratch)

    vm = pl.BlockSpec(memory_space=pltpu.VMEM)
    return pl.pallas_call(
        kernel,
        out_shape=(jax.ShapeDtypeStruct((2, 64, 128), F32), jax.ShapeDtypeStruct((64, CHI), F32)),
        in_specs=[vm, vm],
        out_specs=(vm, vm),
        scratch_shapes=SCRATCH,
        compiler_params=pltpu.CompilerParams(vmem_limit_bytes=24 << 20),
    )(gram, grown)


def shards(left_factor, boundary_site, double_layer):
    highest = lax.Precision.HIGHEST
    absorbed = jnp.einsum(
        "kur,ue->ker", boundary_site.astype(F32), double_layer, precision=highest
    ).astype(BF16)
    part = jnp.einsum("ik,ker->eir", left_factor, absorbed, preferred_element_type=F32)
    grown, gram = gather_call(part, (8, 8, 8))
    return factor_call(gram, grown, lambda: lax.axis_index("lb"))


def solution(mesh):
    return jax.shard_map(
        shards,
        mesh=mesh,
        in_specs=(P("lb", "rep"), P("rep", None, "rb"), P()),
        out_specs=(P("rep", "lb", "rb"), P("lb", None)),
        check_vma=False,
    )
```

```python
import jax
import jax.numpy as jnp
from jax import lax
from jax.experimental import pallas as pl
from jax.experimental.pallas import tpu as pltpu
from jax.sharding import PartitionSpec as P

CHI = 1024
BLOCK = 128
BLOCKS = CHI // BLOCK
TILES = BLOCK // 8
F32 = jnp.float32
BF16 = jnp.bfloat16
NT = (((1,), (1,)), ((), ()))
NN = (((1,), (0,)), ((), ()))


def dot(a, b, dims):
    return lax.dot_general(a, b, dims, precision=lax.Precision.HIGHEST, preferred_element_type=F32)


def mul(a, b, dims):
    return lax.dot_general(a, b, dims, preferred_element_type=F32)


def split(x):
    high = x.astype(BF16)
    rest = x - high.astype(F32)
    middle = rest.astype(BF16)
    return high, middle, (rest - middle.astype(F32)).astype(BF16)


def first(x):
    h, m, l = split(x)
    return jnp.concatenate([h, h, m, m, h, l], axis=1)


def second(x, axis):
    h, m, l = split(x)
    return jnp.concatenate([h, m, h, m, l, h], axis=axis)


def factor_block(r_ref, shadows):
    sub = lax.broadcasted_iota(jnp.int32, (8, BLOCK), 0)
    shadows = list(shadows)
    share = -(-len(shadows) // TILES)

    def spread(tile, row):
        return jnp.broadcast_to(tile[row : row + 1, :], (8, BLOCK))

    def lane(tile, at):
        return jnp.broadcast_to(tile[:, at : at + 1], (8, BLOCK))

    coming = []
    for t in range(TILES):
        at = pl.ds(8 * t, 8)
        left, right = r_ref[at, :BLOCK], r_ref[at, BLOCK:]
        cols = coming if t else [lane(left, n) for n in range(8)]
        roots, lefts, rights, links = [], [], [], []
        scale = jnp.zeros((8, BLOCK), F32)
        pivot = spread(cols[0], 0)
        for i in range(8):
            root = lax.rsqrt(pivot)
            scale = jnp.where(sub == i, root, scale)
            below = jnp.where(sub > i, cols[i], 0.0) * root
            ul, ur = spread(left, i) * root, spread(right, i) * root
            link = {n: spread(cols[n], i) * root for n in range(i + 1, 8)}
            if i < 7:
                pivot = spread(cols[i + 1], i + 1) - link[i + 1] * link[i + 1]
            for n in range(i + 1, 8):
                cols[n] = cols[n] - below * link[n]
            left, right = left - below * ul, right - below * ur
            roots.append(root)
            lefts.append(ul)
            rights.append(ur)
            links.append(link)
        r_ref[at, BLOCK:] = right * scale
        for s in range(t + 1, TILES):
            low = pl.ds(8 * s, 8)
            left, right = r_ref[low, :BLOCK], r_ref[low, BLOCK:]
            cols = [lane(left, 8 * t + n) for n in range(8)]
            if s == t + 1:
                coming = [lane(left, 8 * s + n) for n in range(8)]
            for i in range(8):
                below = cols[i] * roots[i]
                if s == t + 1:
                    coming = [coming[n] - below * spread(below, n) for n in range(8)]
                for n in range(i + 1, 8):
                    cols[n] = cols[n] - below * links[i][n]
                left, right = left - below * lefts[i], right - below * rights[i]
            r_ref[low, :BLOCK] = left
            r_ref[low, BLOCK:] = right
        for shadow in shadows[t * share : (t + 1) * share]:
            shadow()


def factor_kernel(lb_fn, a_ref, g_ref, q_ref, f_ref, r_ref, c_ref, pa_ref, pb_ref, y_ref, ia_ref, ib_ref):
    row = lax.broadcasted_iota(jnp.int32, (BLOCK, BLOCK), 0)
    col = lax.broadcasted_iota(jnp.int32, (BLOCK, BLOCK), 1)
    one = jnp.where(row == col, 1.0, 0.0).astype(F32)

    def block(j):
        return pl.ds(pl.multiple_of(j * BLOCK, BLOCK), BLOCK)

    def chunk(i):
        return slice(256 * i, 256 * i + 256)

    def keep_inverse():
        inv = jnp.where(row >= col, r_ref[:, BLOCK:], 0.0)
        ia_ref[...] = first(inv)
        ib_ref[...] = second(inv, 1)

    def column(j, i):
        def run():
            p = mul(c_ref[chunk(i), :], ib_ref[...], NT)
            rows = 256 * i + lax.broadcasted_iota(jnp.int32, (256, BLOCK), 0)
            cols = j * BLOCK + lax.broadcasted_iota(jnp.int32, (256, BLOCK), 1)
            a_ref[chunk(i), block(j)] = jnp.where(rows >= cols, p, 0.0)
            h, m, l = split(jnp.where(rows >= (j + 1) * BLOCK, p, 0.0))
            pa_ref[chunk(i), :] = jnp.concatenate([h, h, m, m, h, l], axis=1)
            pb_ref[chunk(i), :] = jnp.concatenate([h, m, h, m, l, h], axis=1)
        return run

    def solve(j, h):
        def run():
            y = mul(ia_ref[...], second(g_ref[h, block(j), :], 0), NN)
            g_ref[h, block(j), :] = y
            y_ref[h] = second(y, 0)
        return run

    def ahead(j, i):
        def run():
            c = a_ref[chunk(i), block(j + 1)] - mul(pa_ref[chunk(i), :], pb_ref[block(j + 1), :], NT)
            c_ref[chunk(i), :] = first(c)
        return run

    def trail(k, i):
        def run():
            lo = max(256 * i, BLOCK * k)
            rows = slice(lo, 256 * i + 256)
            cols = slice(BLOCK * k, BLOCK * k + BLOCK)
            a_ref[rows, cols] -= mul(pa_ref[rows, :], pb_ref[cols, :], NT)
        return run

    def sweep(h, i):
        def run():
            at = slice(max(256 * i, BLOCK), 256 * i + 256)
            g_ref[h, at, :] -= mul(pa_ref[at, :], y_ref[h], NN)
        return run

    r_ref[:, :BLOCK] = a_ref[:BLOCK, :BLOCK]
    r_ref[:, BLOCK:] = one
    factor_block(r_ref, [])
    keep_inverse()
    for i in range(4):
        c_ref[chunk(i), :] = first(a_ref[chunk(i), :BLOCK])

    def body(j, carry):
        p = mul(c_ref[block(j + 1), :], ib_ref[...], NT)
        r_ref[:, :BLOCK] = a_ref[block(j + 1), block(j + 1)] - mul(first(p), second(p, 1), NT)
        r_ref[:, BLOCK:] = one
        shadows = [column(j, i) for i in range(4)] + [solve(j, h) for h in range(2)] + [ahead(j, i) for i in range(4)]
        shadows += [trail(k, i) for k in range(2, BLOCKS) for i in range(k // 2, 4)]
        shadows += [sweep(h, i) for h in range(2) for i in range(4)]
        factor_block(r_ref, shadows)
        keep_inverse()
        return carry

    lax.fori_loop(0, BLOCKS - 1, body, 0)
    for i in range(4):
        column(BLOCKS - 1, i)()
    for h in range(2):
        solve(BLOCKS - 1, h)()
    lb = lb_fn()
    at = pl.ds(pl.multiple_of(lb * 64, 64), 64)
    for h in range(2):
        q_ref[h] = g_ref[h, at, :] * 128.0
    f_ref[...] = a_ref[at, :] * (1.0 / 128.0)


SCRATCH = [
    pltpu.VMEM((CHI, CHI), F32),
    pltpu.VMEM((2, CHI, BLOCK), F32),
    pltpu.VMEM((BLOCK, 2 * BLOCK), F32),
    pltpu.VMEM((CHI, 6 * BLOCK), BF16),
    pltpu.VMEM((CHI, 6 * BLOCK), BF16),
    pltpu.VMEM((CHI, 6 * BLOCK), BF16),
    pltpu.VMEM((2, 6 * BLOCK, BLOCK), BF16),
    pltpu.VMEM((BLOCK, 6 * BLOCK), BF16),
    pltpu.VMEM((BLOCK, 6 * BLOCK), BF16),
]


MESH = pl.DeviceIdType.MESH


def mod(value, size):
    return lax.rem(value + 2 * size, size)


def gather_kernel(sizes, part_ref, grown_ref, gram_ref, a_recv, joined, products, z_recv, total, y_recv, tile, sems):
    nx, nz, ny = sizes
    lb, z, y = lax.axis_index("lb"), lax.axis_index("rb"), lax.axis_index("rep")
    x, core = lb // 2, lax.rem(lb, 2)
    half = nx // 2
    (a_send, a_got, b_send, b_got, p_send, p_got, c_send, c_got, d_send, d_got,
     e_send, e_got, f_send, f_got, g_send, g_got, h_send, h_got) = sems

    def remote(src, dst, send, got, target):
        return pltpu.make_async_remote_copy(
            src_ref=src, dst_ref=dst, send_sem=send, recv_sem=got, device_id=target, device_id_type=MESH
        )

    barrier = pltpu.get_barrier_semaphore()
    for d in range(1, ny):
        pl.semaphore_signal(barrier, inc=1, device_id={"rep": mod(y + d, ny)}, device_id_type=MESH)
    for d in range(1, nz):
        pl.semaphore_signal(barrier, inc=1, device_id={"rb": mod(z + d, nz)}, device_id_type=MESH)
    for d in range(1, 2 * nx):
        pl.semaphore_signal(barrier, inc=1, device_id={"lb": mod(lb + d, 2 * nx)}, device_id_type=MESH)
    pl.semaphore_wait(barrier, ny - 1 + nz - 1 + 2 * nx - 1)

    def far_first(n):
        return sorted(range(1, n), key=lambda d: -min(d, n - d))

    rows = pl.ds(pl.multiple_of(lb * 64, 64), 64)
    sent = []

    def near_first(n):
        return sorted(range(1, n), key=lambda d: min(d, n - d))

    opposite = ny // 2
    arriving = {}

    def deliver(e, d, src):
        at = e * (ny - 1) + d - 1
        copy = remote(src, a_recv.at[at], a_send.at[at], a_got.at[at], {"rep": mod(y + d, ny)})
        copy.start()
        arriving[e, d] = copy
        sent.append(copy)

    handing = []
    for e, turn in ((0, 1), (1, -1)):
        src = part_ref.at[2 * mod(y + opposite, ny) + e]
        at = e * (ny - 1) + opposite - 1
        copy = remote(src, a_recv.at[at], a_send.at[at], a_got.at[at], {"rep": mod(y + turn, ny)})
        copy.start()
        handing.append(copy)
        sent.append(copy)
    for e, turn in ((0, 1), (1, -1)):
        late = (opposite - turn) % ny
        for d in far_first(ny):
            if d not in (opposite, late):
                deliver(e, d, part_ref.at[2 * mod(y + d, ny) + e])
        handing[e].wait_recv()
        joined[e] = a_recv[e * (ny - 1) + opposite - 1] + part_ref[2 * mod(y + late, ny) + e]
        deliver(e, late, joined.at[e])

    def settle(e):
        mine = part_ref[2 * y + e]
        late = opposite - 1 if e == 0 else opposite + 1
        for d in [d for d in near_first(ny) if d not in (opposite, late)] + [late]:
            arriving[e, d].wait_recv()
            mine = mine + a_recv[e * (ny - 1) + d - 1]
        grown_ref[e, rows, :] = mine

    def block(e, chip, which):
        return grown_ref.at[e, pl.ds(pl.multiple_of((2 * chip + which) * 64, 64), 64)]

    partner = {"lb": 2 * x + 1 - core}
    handed = {}

    def hand(e, step, direction):
        chip = mod(x - direction * step, nx)
        slot = ((0 if direction > 0 else 1) * (half + 1) + step) * 2 + e
        copy = remote(block(e, chip, core), block(e, chip, core), p_send.at[slot], p_got.at[slot], partner)
        copy.start()
        handed[direction, step, e] = copy
        sent.append(copy)

    flying = {}

    def ring(direction, step, e):
        chip = mod(x - direction * (step - 1), nx)
        slot = ((0 if direction > 0 else 1) * half + step - 1) * 2 + e
        to = {"lb": 2 * mod(x + direction, nx) + core}
        copy = remote(block(e, chip, core), block(e, chip, core), b_send.at[slot], b_got.at[slot], to)
        copy.start()
        flying[direction, step, e] = copy
        sent.append(copy)

    def ways(step, e):
        return (1, -1) if step < half else ((1,) if e == 0 else (-1,))

    def launch(e):
        for direction in ways(1, e):
            ring(direction, 1, e)
        hand(e, 0, 1)

    def advance(step, e):
        for direction in ways(step, e):
            flying[direction, step, e].wait_recv()
            if step < half and direction in ways(step + 1, e):
                ring(direction, step + 1, e)
            hand(e, step, direction)

    def product(chip):
        at = pl.ds(pl.multiple_of(chip * 128, 128), 128)
        ours = [grown_ref[e, rows, :] for e in range(2)]
        products[chip] = dot(ours[0], grown_ref[0, at, :], NT) + dot(ours[1], grown_ref[1, at, :], NT)

        @pl.when(chip != z)
        def _():
            remote(products.at[chip], z_recv.at[z], c_send.at[chip], c_got.at[z], {"rb": chip}).start()

    settle(0)
    launch(0)
    advance(1, 0)
    settle(1)
    launch(1)
    for e in range(2):
        handed[1, 0, e].wait_recv()
    product(x)
    for step in range(1, half + 1):
        if step > 1:
            advance(step, 0)
        advance(step, 1)
        if step < half:
            for direction in (1, -1):
                for e in range(2):
                    handed[direction, step, e].wait_recv()
                product(mod(x - direction * step, nx))
    handed[1, half, 0].wait_recv()
    handed[-1, half, 1].wait_recv()
    product(mod(x + half, nx))
    summed = products[z]
    for d in near_first(nz):
        far = mod(z + d, nz)
        copy = remote(products.at[far], z_recv.at[far], c_send.at[far], c_got.at[far], {"rb": far})
        copy.wait_recv()
        summed = summed + z_recv[far]
        sent.append(copy)
    total[...] = summed
    copies = []
    for d in far_first(ny):
        to = mod(y + d, ny)
        src = total.at[pl.ds(pl.multiple_of(8 * to, 8), 8)]
        copy = remote(src, y_recv.at[d - 1], d_send.at[d - 1], d_got.at[d - 1], {"rep": to})
        copy.start()
        copies.append((d, copy))
    summed = total[pl.ds(pl.multiple_of(8 * y, 8), 8), :]
    for d, copy in sorted(copies, key=lambda pair: min(pair[0], ny - pair[0])):
        copy.wait_recv()
        summed = summed + y_recv[d - 1]
    tile[...] = summed
    sent += [copy for _, copy in copies]

    def place(which):
        return z * (1 - which) + y * which, y * (1 - which) + z * which

    side = lb // nx
    outer, inner = place(side)
    spot = lax.rem(lb, nx)
    home = gram_ref.at[side, outer, inner, pl.ds(pl.multiple_of(8 * spot, 8), 8)]
    copies = []
    for d in far_first(nx):
        copy = remote(tile, home, e_send.at[d], e_got.at[spot], {"lb": 2 * mod(x + d, nx) + side})
        copy.start()
        copies.append(copy)
    across = remote(tile, home, e_send.at[0], e_got.at[spot], partner)
    here = pltpu.make_async_copy(tile, home, e_got.at[spot])

    @pl.when(core == side)
    def _():
        here.start()

    @pl.when(core != side)
    def _():
        across.start()
        across.wait_send()

    sent += copies
    outer, inner = place(core)
    for i in range(nx):
        landed = gram_ref.at[core, outer, inner, pl.ds(8 * i, 8)]
        pltpu.make_async_copy(tile, landed, e_got.at[i]).wait()

    n = ny
    chunk = gram_ref.at[core, outer, inner]
    for d in far_first(n):
        to = {"rep": mod(y + d * (1 - core), n), "rb": mod(z + d * core, n)}
        copy = remote(chunk, chunk, f_send.at[d], f_got.at[inner], to)
        copy.start()
        sent.append(copy)

    def gathered(position):
        @pl.when(position != inner)
        def _():
            remote(chunk, chunk, f_send.at[0], f_got.at[position], partner).wait_recv()

    cuts = 4
    width = n // cuts
    middle = n // 2

    def piece(position, cut):
        return gram_ref.at[core, position, pl.ds(cut * width, width)]

    def around(direction, step, cut):
        position = mod(outer - direction * (step - 1), n)
        slot = ((0 if direction > 0 else 1) * middle + step - 1) * cuts + cut
        to = {"rb": mod(z + direction * (1 - core), n), "rep": mod(y + direction * core, n)}
        copy = remote(piece(position, cut), piece(position, cut), g_send.at[slot], g_got.at[slot], to)
        copy.start()
        sent.append(copy)
        return copy

    handed = []

    def share(position, cut, slot):
        copy = remote(piece(position, cut), piece(position, cut), h_send.at[slot], h_got.at[slot], partner)
        copy.start()
        handed.append(copy)

    def turns(step):
        if step < middle:
            return [(direction, cut) for cut in range(cuts) for direction in (1, -1)]
        return [(1 if cut < cuts // 2 else -1, cut) for cut in (0, cuts // 2, 1, cuts // 2 + 1)]

    flying = {}
    for cut in range(cuts):
        for position in range(cut * width, cut * width + width):
            gathered(position)
        for direction in (1, -1):
            flying[direction, 1, cut] = around(direction, 1, cut)
        share(outer, cut, cut)
    slot = cuts
    for step in range(1, middle + 1):
        for direction, cut in turns(step):
            flying[direction, step, cut].wait_recv()
            if step < middle and (direction, cut) in turns(step + 1):
                flying[direction, step + 1, cut] = around(direction, step + 1, cut)
            share(mod(outer - direction * step, n), cut, slot)
            slot += 1
    for copy in handed:
        copy.wait_recv()
    for copy in sent + handed:
        copy.wait_send()


def gather_call(part, sizes):
    nx, nz, ny = sizes
    vm = pl.BlockSpec(memory_space=pltpu.VMEM)
    counts = [2 * (ny - 1)] * 2 + [2 * nx] * 2 + [2 * nx + 4] * 2 + [nz] * 2 + [ny - 1] * 2 + [nx] * 2 + [ny] * 2 + [4 * ny] * 4

    def kernel(part_ref, grown_ref, gram_ref, a_recv, joined, products, z_recv, total, y_recv, tile, *sems):
        gather_kernel(sizes, part_ref, grown_ref, gram_ref, a_recv, joined, products, z_recv, total, y_recv, tile, sems)

    return pl.pallas_call(
        kernel,
        out_shape=(
            jax.ShapeDtypeStruct((2, 128 * nx, 128), F32),
            jax.ShapeDtypeStruct((2, ny, ny, 8 * nx, 128), F32),
        ),
        in_specs=[vm],
        out_specs=(vm, vm),
        scratch_shapes=[
            pltpu.VMEM((2 * (ny - 1), 64, 128), F32),
            pltpu.VMEM((2, 64, 128), F32),
            pltpu.VMEM((nz, 64, 128), F32),
            pltpu.VMEM((nz, 64, 128), F32),
            pltpu.VMEM((64, 128), F32),
            pltpu.VMEM((ny - 1, 8, 128), F32),
            pltpu.VMEM((8, 128), F32),
        ]
        + [pltpu.SemaphoreType.DMA((count,)) for count in counts],
        compiler_params=pltpu.CompilerParams(collective_id=0, has_side_effects=True, vmem_limit_bytes=24 << 20),
    )(part)


def factor_call(gram, grown, lb_fn):
    def kernel(a_in, g_in, q_ref, f_ref, a_ref, g_ref, *scratch):
        for outer in range(8):
            for inner in range(8):
                for i in range(8):
                    at = pl.ds(8 * i, 8)
                    up, low = 64 * i + 8 * inner, 512 + 64 * i + 8 * outer
                    a_ref[up : up + 8, 128 * outer : 128 * outer + 128] = a_in[0, outer, inner, at, :]
                    a_ref[low : low + 8, 128 * inner : 128 * inner + 128] = a_in[1, outer, inner, at, :]
        g_ref[...] = g_in[...]
        factor_kernel(lb_fn, a_ref, g_ref, q_ref, f_ref, *scratch)

    vm = pl.BlockSpec(memory_space=pltpu.VMEM)
    return pl.pallas_call(
        kernel,
        out_shape=(jax.ShapeDtypeStruct((2, 64, 128), F32), jax.ShapeDtypeStruct((64, CHI), F32)),
        in_specs=[vm, vm],
        out_specs=(vm, vm),
        scratch_shapes=SCRATCH,
        compiler_params=pltpu.CompilerParams(vmem_limit_bytes=24 << 20),
    )(gram, grown)


def shards(left_factor, boundary_site, double_layer):
    highest = lax.Precision.HIGHEST
    absorbed = jnp.einsum(
        "kur,ue->ker", boundary_site.astype(F32), double_layer, precision=highest
    ).astype(BF16)
    part = jnp.einsum("ik,ker->eir", left_factor, absorbed, preferred_element_type=F32)
    grown, gram = gather_call(part, (8, 8, 8))
    return factor_call(gram, grown, lambda: lax.axis_index("lb"))


def solution(mesh):
    return jax.shard_map(
        shards,
        mesh=mesh,
        in_specs=(P("lb", "rep"), P("rep", None, "rb"), P()),
        out_specs=(P("rep", "lb", "rb"), P("lb", None)),
        check_vma=False,
    )
```
